32 devices in a mesh: dp: 8 (over y, x, core), mp: 4 (over z).
Axes of the slice: x: 2, y: 2, z: 4, core: 2. Of those that a mesh axis runs over, the one named last changes fastest.
Arguments:
- hidden_in: bfloat16 [2, 8192, 2048], P(None, ('dp', 'mp')), may hold values from -6 to 6
- counts: int32 [2, 8], P(None, 'dp'), may hold values from 20 to 50, as said below
- summary: float32 [50, 2048], replicated, may hold values from -6 to 6
- query_weight: bfloat16 [2048, 2048], P('dp', 'mp'), may hold values from -0.125 to 0.125
- query_bias: bfloat16 [2048], P('mp'), may hold values from -1.75 to 1.75
- key_weight: bfloat16 [2048, 2048], P('dp', 'mp'), may hold values from -0.125 to 0.125
- value_weight: bfloat16 [2048, 2048], P('dp', 'mp'), may hold values from -0.125 to 0.125
- value_bias: bfloat16 [2048], P('mp'), may hold values from -1.75 to 1.75
- out_weight: bfloat16 [2048, 2048], P('mp', 'dp'), may hold values from -2 to 2
- out_bias: bfloat16 [2048], replicated, may hold values from -1.25 to 1.25
- up_weight: bfloat16 [2048, 8192], P('dp', 'mp'), may hold values from -0.125 to 0.125
- up_bias: bfloat16 [8192], P('mp'), may hold values from -1.75 to 1.75
- down_weight: bfloat16 [8192, 2048], P('mp', 'dp'), may hold values from -0.0625 to 0.0625
- down_bias: bfloat16 [2048], replicated, may hold values from -1.25 to 1.25
- attn_gain: float32 [2048], replicated, may hold values from 0.5 to 1.5
- attn_shift: float32 [2048], replicated, may hold values from -0.625 to 0.625
- mlp_gain: float32 [2048], replicated, may hold values from 0.5 to 1.5
- mlp_shift: float32 [2048], replicated, may hold values from -0.625 to 0.625
- cotangent: bfloat16 [2, 8192, 2048], P(None, ('dp', 'mp')), may hold values from -6 to 6
Outputs:
- layer_out: bfloat16 [2, 8192, 2048], P(None, ('dp', 'mp'))
- grad_input: float32 [2, 8192, 2048], P(None, ('dp', 'mp'))
- grad_summary: float32 [50, 2048], replicated
- grad_query_weight: float32 [2048, 2048], P('dp', 'mp')
- grad_query_bias: float32 [2048], P('mp')
- grad_key_weight: float32 [2048, 2048], P('dp', 'mp')
- grad_value_weight: float32 [2048, 2048], P('dp', 'mp')
- grad_value_bias: float32 [2048], P('mp')
- grad_out_weight: float32 [2048, 2048], P('mp', 'dp')
- grad_out_bias: float32 [2048], replicated
- grad_up_weight: float32 [2048, 8192], P('dp', 'mp')
- grad_up_bias: float32 [8192], P('mp')
- grad_down_weight: float32 [8192, 2048], P('mp', 'dp')
- grad_down_bias: float32 [2048], replicated
- grad_attn_gain: float32 [2048], replicated
- grad_attn_shift: float32 [2048], replicated
- grad_mlp_gain: float32 [2048], replicated
- grad_mlp_shift: float32 [2048], replicated
The draws below stay inside these ranges and needn't reach their ends.
Inputs may be any that keep to these rules, and one draw needn't show every extreme that they name: `counts`: an item's count c marks the first c of its 50 prefix slots and the first c of its 50 appended slots as used.
All inputs are finite; a program needn't handle non-finite values.
Results may differ from the reference program's by a relative error of at most 0.02.
Values may be sent and summed in bfloat16 or wider, within the bound.
No kernel may reach another device: no remote copies, remote signals or barrier semaphores. Data moves between devices by JAX's collectives and lax.ppermute only.
A program may use at most 256 MiB of HBM per device.

```python
import jax
import jax.numpy as jnp
from jax import lax

D = 2048
HEADS = 32
HD = 64
FF = 8192
SUMM = 50
MB = 2
SEQ = 1024
ROWS = 8192
N_DP = 8


def draw_counts(key, part):
    drawn = jax.random.randint(jax.random.fold_in(key, 11), (MB * N_DP,), 2 * SUMM // 5, SUMM + 1, dtype=jnp.int32)
    places = jax.random.permutation(jax.random.fold_in(key, 12), MB * N_DP)
    drawn = drawn.at[places[0]].set(SUMM)
    drawn = drawn.at[places[1]].set(2 * SUMM // 5)
    return drawn.reshape(MB, N_DP)


def shard_levels(rng, dims, pieces, low, largest):
    level = 1.0
    for dim, parts in pieces:
        heights = jax.random.uniform(jax.random.fold_in(jax.random.fold_in(rng, 6), dim), (parts,), jnp.float32, low / len(pieces), largest / len(pieces))
        level = level * jnp.repeat(jnp.exp(heights), dims[dim] // parts).reshape((-1,) + (1,) * (len(dims) - 1 - dim))
    return level


def normal_values(key, extent, scale, limit, cuts=(), held_as=jnp.bfloat16):
    values = jax.random.normal(key, extent, jnp.float32) * scale
    if len(cuts) > 0:
        values = shard_levels(key, extent, cuts, -0.22, 0.18) * values
    return jnp.clip(values, min=-limit, max=limit).astype(held_as)


def setup_inputs(seed: int = 0) -> dict:
    seeds = jax.random.split(jax.random.key(seed), 20)
    return {
        "hidden_in": normal_values(seeds[0], (MB, ROWS, D), 1.0, 6.0, ((1, 32),)),
        "counts": draw_counts(jax.random.fold_in(seeds[19], 71), 0),
        "summary": normal_values(seeds[2], (SUMM, D), 1.0, 6.0, (), jnp.float32),
        "query_weight": normal_values(seeds[3], (D, D), D ** -0.5, 0.125, ((0, 8), (1, 4))),
        "query_bias": normal_values(seeds[4], (D,), 0.3, 1.75, ((0, 4),)),
        "key_weight": normal_values(seeds[5], (D, D), D ** -0.5, 0.125, ((0, 8), (1, 4))),
        "value_weight": normal_values(seeds[6], (D, D), D ** -0.5, 0.125, ((0, 8), (1, 4))),
        "value_bias": normal_values(seeds[7], (D,), 0.3, 1.75, ((0, 4),)),
        "out_weight": normal_values(seeds[8], (D, D), (max(4 * D // SEQ, 1)) ** -0.5, 2.0, ((0, 4), (1, 8))),
        "out_bias": normal_values(seeds[9], (D,), 0.2, 1.25),
        "up_weight": normal_values(seeds[10], (D, FF), D ** -0.5, 0.125, ((0, 8), (1, 4))),
        "up_bias": normal_values(seeds[11], (FF,), 0.3, 1.75, ((0, 4),)),
        "down_weight": normal_values(seeds[12], (FF, D), FF ** -0.5, 0.0625, ((0, 4), (1, 8))),
        "down_bias": normal_values(seeds[13], (D,), 0.2, 1.25),
        "attn_gain": jnp.clip(1.0 + 0.1 * jax.random.normal(seeds[14], (D,), jnp.float32), 0.5, 1.5),
        "attn_shift": normal_values(seeds[15], (D,), 0.1, 0.625, (), jnp.float32),
        "mlp_gain": jnp.clip(1.0 + 0.1 * jax.random.normal(seeds[16], (D,), jnp.float32), 0.5, 1.5),
        "mlp_shift": normal_values(seeds[17], (D,), 0.1, 0.625, (), jnp.float32),
        "cotangent": normal_values(seeds[18], (MB, ROWS, D), 1.0, 6.0, ((1, 32),)),
    }


precise = lax.Precision.HIGHEST

@jax.custom_vjp
def low(v):
    return lax.optimization_barrier(v.astype(jnp.bfloat16)).astype(jnp.float32)

@jax.custom_vjp
def low_back(v):
    return v

def low_keep(v):
    return (low(v), None)

def low_pass(kept, grad):
    return (grad,)

def back_keep(v):
    return (v, None)

def back_low(kept, grad):
    return (low(grad),)
low.defvjp(low_keep, low_pass)
low_back.defvjp(back_keep, back_low)

def layer_norm(values_in, gain_vec, shift_vec):
    centred = values_in - lax.optimization_barrier(jnp.mean(values_in, axis=-1, keepdims=True))
    spread = lax.optimization_barrier(jnp.mean(centred * centred, axis=-1, keepdims=True))
    return centred * lax.rsqrt(spread + 1e-05) * gain_vec + shift_vec

def matmul(left_side, right_side):
    return jnp.dot(left_side, right_side, precision=precise)

def attend(query_rows, key_rows, value_rows, allowed):
    scores = low_back(jnp.einsum('qhd,khd->hqk', query_rows, key_rows, precision=precise))
    scores = jnp.where(allowed[None], scores, -1e+30)
    weights_low = low(jax.nn.softmax(scores, axis=-1))
    return jnp.einsum('hqk,khd->qhd', weights_low, value_rows, precision=precise)

def item_forward(x_item, item_count, summary, query_weight, query_bias, key_weight, value_weight, value_bias, out_weight, out_bias, up_weight, up_bias, down_weight, down_bias, attn_gain, attn_shift, mlp_gain, mlp_shift):
    positions = jnp.arange(SEQ, dtype=jnp.int32)
    slot_ids = positions - (SEQ - SUMM)
    picker = (slot_ids[:, None] == jnp.arange(SUMM, dtype=jnp.int32)[None, :]).astype(jnp.float32)
    joined = x_item + matmul(picker, summary)
    normed = low(layer_norm(joined, attn_gain, attn_shift))
    query_rows = low_back(low((matmul(normed, query_weight) + query_bias) * HD ** (-0.5)))
    key_rows = low_back(low(matmul(normed, key_weight)))
    value_rows = low_back(low(matmul(normed, value_weight) + value_bias))
    key_live = (positions >= SUMM) & (slot_ids < 0) | (positions < item_count) | (slot_ids >= 0) & (slot_ids < item_count)
    allowed = (positions[None, :] <= positions[:, None]) & key_live[None, :]
    attended = jax.checkpoint(attend)(query_rows.reshape(SEQ, HEADS, HD), key_rows.reshape(SEQ, HEADS, HD), value_rows.reshape(SEQ, HEADS, HD), allowed).reshape(SEQ, D)
    attended = low_back(low(attended))
    mixed_rows = joined + low_back(matmul(attended, out_weight)) + out_bias
    normed_two = low(layer_norm(mixed_rows, mlp_gain, mlp_shift))
    up_value = low_back(matmul(normed_two, up_weight) + up_bias)
    active = low(jax.nn.gelu(up_value, approximate=True))
    return mixed_rows + low_back(matmul(active, down_weight)) + down_bias

def reference(hidden_in, counts, summary, query_weight, query_bias, key_weight, value_weight, value_bias, out_weight, out_bias, up_weight, up_bias, down_weight, down_bias, attn_gain, attn_shift, mlp_gain, mlp_shift, cotangent):
    weights = jax.tree.map(lambda array: array.astype(jnp.float32), (summary, query_weight, query_bias, key_weight, value_weight, value_bias, out_weight, out_bias, up_weight, up_bias, down_weight, down_bias, attn_gain, attn_shift, mlp_gain, mlp_shift))
    inputs = hidden_in.astype(jnp.float32).reshape(MB * N_DP, SEQ, D)
    grads_in = cotangent.astype(jnp.float32).reshape(MB * N_DP, SEQ, D)
    item_counts = counts.reshape(MB * N_DP).astype(jnp.int32)

    def one_item(totals, packed):
        x_item, item_count, grad_item = packed

        def forward(x_value, *params):
            return item_forward(x_value, item_count, *params)
        result, pullback = jax.vjp(forward, x_item, *weights)
        pulled = pullback(grad_item)
        totals = jax.tree.map(jnp.add, totals, tuple(pulled[1:]))
        return (totals, (result, pulled[0]))
    zero_sums = jax.tree.map(jnp.zeros_like, weights)
    totals, (results, grad_rows) = lax.scan(one_item, zero_sums, (inputs, item_counts, grads_in))
    layer_out = results.reshape(MB, N_DP * SEQ, D).astype(jnp.bfloat16)
    grad_input = grad_rows.reshape(MB, N_DP * SEQ, D)
    return (layer_out, grad_input, totals[0], totals[1], totals[2], totals[3], totals[4], totals[5], totals[6], totals[7], totals[8], totals[9], totals[10], totals[11], totals[12], totals[13], totals[14], totals[15])
```

```python
import functools
import math

import jax
import jax.numpy as jnp
from jax import lax
from jax.experimental import pallas as pl
from jax.experimental.pallas import tpu as pltpu
from jax.sharding import Mesh
from jax.sharding import PartitionSpec as P

D = 2048
HD = 64
SUMM = 50

precise = lax.Precision.HIGHEST
gelu_coef = math.sqrt(2.0 / math.pi)
bf16 = jnp.bfloat16
f32 = jnp.float32
DP = ("xy", "c")
MP = ("g", "r")
ALL = ("xy", "c", "g", "r")


def gelu_pair(v):
    inner = gelu_coef * (v + 0.044715 * v * v * v)
    tangent = jnp.tanh(inner)
    half = 0.5 * (1.0 + tangent)
    slope = half + 0.5 * v * (1.0 - tangent * tangent) * gelu_coef * (1.0 + 3.0 * 0.044715 * v * v)
    return v * half, slope


def layer_norm(values_in, gain_vec, shift_vec):
    centred = values_in - jnp.mean(values_in, axis=-1, keepdims=True)
    spread = jnp.mean(centred * centred, axis=-1, keepdims=True)
    scaled = lax.rsqrt(spread + 1e-05)
    unit_rows = centred * scaled
    return (unit_rows * gain_vec + shift_vec, unit_rows, scaled)


def norm_back(grad_out, unit_rows, scaled, gain_vec):
    weighted = grad_out * gain_vec
    return scaled * (
        weighted
        - jnp.mean(weighted, axis=-1, keepdims=True)
        - unit_rows * jnp.mean(weighted * unit_rows, axis=-1, keepdims=True)
    )


def dense(left_side, right_side):
    return jnp.dot(left_side, right_side, preferred_element_type=f32)


def times_t(left_side, right_side):
    return lax.dot_general(left_side, right_side, (((1,), (1,)), ((), ())), preferred_element_type=f32)


def inner_rows(left_side, right_side):
    return lax.dot_general(left_side, right_side, (((0,), (0,)), ((), ())), preferred_element_type=f32)


def live_keys(positions, seq_len, item_count):
    slot_ids = positions - (seq_len - SUMM)
    return (
        (positions >= SUMM) & (slot_ids < 0)
        | (positions >= 0) & (positions < item_count)
        | (slot_ids >= 0) & (slot_ids < item_count)
    )


def swap_pair(values):
    return lax.ppermute(values, "r", [(0, 1), (1, 0)])


def swap_core(values):
    return lax.ppermute(values, "c", [(0, 1), (1, 0)])


def shift_up(values, step):
    size = lax.axis_size("g")
    return lax.ppermute(values, "g", [(i, i + step) for i in range(size - step)])


def shift_down(values, step):
    size = lax.axis_size("g")
    return lax.ppermute(values, "g", [(i + step, i) for i in range(size - step)])


def turn_up(values, step):
    size = lax.axis_size("g")
    return lax.ppermute(values, "g", [(i, (i + step) % size) for i in range(size)])


def turn_down(values, step):
    size = lax.axis_size("g")
    return lax.ppermute(values, "g", [((i + step) % size, i) for i in range(size)])


def cost(work, size):
    return pl.CostEstimate(flops=int(1 * work), bytes_accessed=int(1 * size), transcendentals=0)


def after(values, *earlier):
    return lax.optimization_barrier((values, earlier))[0]


def ring_order():
    size = lax.axis_size("xy")
    return list(range(size // 2)) + list(range(size - 1, size // 2 - 1, -1))


def ring_step(values, way):
    order = ring_order()
    size = len(order)
    return lax.ppermute(values, "xy", [(order[i], order[(i + way) % size]) for i in range(size)])


def ring_blocks():
    order = ring_order()
    size = len(order)
    here = jnp.asarray([order.index(i) for i in range(size)], jnp.int32)[lax.axis_index("xy")]
    offsets = [0] + [way * step for step in range(1, size // 2) for way in (-1, 1)] + [size // 2]
    chips = jnp.asarray(order, jnp.int32)[(here + jnp.asarray(offsets, jnp.int32)) % size]
    core = lax.axis_index("c")
    return jnp.concatenate((2 * chips + core, 2 * chips + 1 - core))


class RingGather:
    def __init__(self, shard):
        self.blocks = [shard]
        self.right, self.left = ring_step(shard, 1), ring_step(shard, -1)
        self.steps = lax.axis_size("xy") // 2 - 1

    def advance(self, turn):
        while self.steps > 1:
            self.blocks += [self.right, self.left]
            self.right, self.left = ring_step(self.right, 1), ring_step(self.left, -1)
            self.steps -= 1
        self.blocks += [self.right, self.left]
        half = self.right.shape[0] // 2
        right, left = turn(lambda right, left: (right[:half], left[half:]), self.right, self.left)
        self.right, self.left = ring_step(right, 1), ring_step(left, -1)

    def across(self, turn):
        self.mine = turn(lambda *parts: jnp.concatenate(parts), *self.blocks, self.right, self.left)
        self.other = swap_core(self.mine)

    def finish(self, turn):
        return turn(lambda mine, other: jnp.concatenate((mine, other)), self.mine, self.other)


class RingScatter:
    def __init__(self, total, depth):
        self.steps = lax.axis_size("xy") // 2
        self.half = depth // 2
        self.blocks = [total[i * depth : (i + 1) * depth] for i in range(2 * self.steps)]
        self.first = True
        self.send(self.blocks[-1][: self.half], self.blocks[-1][self.half :])

    def send(self, right, left):
        self.steps -= 1
        self.came = (ring_step(right, 1), ring_step(left, -1))

    def add(self, right_block, left_block, right, left):
        def total(block, part):
            return (block.astype(f32) + part.astype(f32)).astype(bf16)

        if not self.first:
            return total(right_block, right), total(left_block, left)
        half = self.half
        return (
            jnp.concatenate((total(right_block[:half], right), right_block[half:])),
            jnp.concatenate((left_block[:half], total(left_block[half:], left))),
        )

    def advance(self, turn):
        right, left = self.blocks[2 * self.steps], self.blocks[2 * self.steps - 1]
        right, left = turn(self.add, right, left, *self.came)
        self.first = False
        self.send(right, left)

    def finish(self, turn):
        while self.steps > 0:
            self.advance(turn)

        def total(block, right, left):
            return (block.astype(f32) + right.astype(f32) + left.astype(f32)).astype(bf16)

        return turn(total, self.blocks[0], *self.came)


def move_block(order_ref, in_ref, out_ref):
    out_ref[...] = in_ref[...]


def pick_columns(values, order):
    rows, columns = values.shape
    width = columns // order.shape[0]
    return pl.pallas_call(
        move_block,
        grid_spec=pltpu.PrefetchScalarGridSpec(
            num_scalar_prefetch=1,
            grid=(order.shape[0],),
            in_specs=[pl.BlockSpec((rows, width), lambda j, order_ref: (0, order_ref[j]))],
            out_specs=pl.BlockSpec((rows, width), lambda j, order_ref: (0, j)),
        ),
        out_shape=jax.ShapeDtypeStruct(values.shape, values.dtype),
        cost_estimate=cost(0, 4 * values.size * values.dtype.itemsize),
        name="pick_columns",
    )(order, values)


class SumAll:
    def __init__(self, values, turn):
        half = values.shape[0] // 2
        core = lax.axis_index("c")
        self.total, other = turn(
            lambda values: (
                lax.dynamic_slice_in_dim(values, core * half, half, 0),
                lax.dynamic_slice_in_dim(values, (1 - core) * half, half, 0),
            ),
            values,
        )
        self.came = swap_core(other)
        self.ways = []
        for axis in ("xy", "r", "g"):
            size = lax.axis_size(axis)
            bit = 1
            while bit < size:
                self.ways.append((axis, [(i, i ^ bit) for i in range(size)]))
                bit *= 2
        self.left = len(self.ways)

    def advance(self, turn):
        self.total = turn(jnp.add, self.total, self.came)
        axis, pairs = self.ways[len(self.ways) - self.left]
        self.came = lax.ppermute(self.total, axis, pairs)
        self.left -= 1

    def finish(self, turn):
        while self.left > 0:
            self.advance(turn)
        self.total = turn(jnp.add, self.total, self.came)
        other = swap_core(self.total)
        low = lax.axis_index("c") == 0
        return turn(
            lambda total, other: jnp.where(
                low, jnp.concatenate((total, other)), jnp.concatenate((other, total))
            ),
            self.total,
            other,
        )


def contract(left, right, dims):
    return lax.dot_general(left, right, (dims, ((), ())), preferred_element_type=f32)


def head_parts(near_ref, far_ref, h):
    query = near_ref[:, h * HD : (h + 1) * HD]
    key = jnp.concatenate((near_ref[:, (2 + h) * HD : (3 + h) * HD], far_ref[:, (2 + h) * HD : (3 + h) * HD]))
    value = jnp.concatenate((near_ref[:, (4 + h) * HD : (5 + h) * HD], far_ref[:, (4 + h) * HD : (5 + h) * HD]))
    return query, key, value


def attend_kernel(row_ref, key_ref, near_ref, far_ref, out_ref, log_ref):
    allowed = key_ref[...] <= row_ref[...]
    outs = []
    for h in range(2):
        query, key, value = head_parts(near_ref, far_ref, h)
        scores = jnp.where(allowed, contract(key, query, ((1,), (1,))), -1e30)
        top = jnp.max(scores, axis=0, keepdims=True)
        powers = jnp.exp(scores - top)
        whole = jnp.sum(powers, axis=0, keepdims=True)
        outs.append(contract(value, powers.astype(bf16), ((0,), (0,))) / whole)
        log_ref[0, h : h + 1, :] = top + jnp.log(whole)
    out_ref[...] = jnp.concatenate(outs, axis=0).T.astype(bf16)


def attend(near, far, row_at, key_mark):
    rows = row_at.shape[0]
    keys = rows + far.shape[0]
    pairs = near.shape[1] // (6 * HD)
    return pl.pallas_call(
        attend_kernel,
        grid=(pairs,),
        in_specs=[
            pl.BlockSpec((1, rows), lambda j: (0, 0)),
            pl.BlockSpec((keys, 1), lambda j: (0, 0)),
            pl.BlockSpec((rows, 6 * HD), lambda j: (0, j)),
            pl.BlockSpec((keys - rows, 6 * HD), lambda j: (0, j)),
        ],
        out_specs=[
            pl.BlockSpec((rows, 2 * HD), lambda j: (0, j)),
            pl.BlockSpec((1, 2, rows), lambda j: (j, 0, 0)),
        ],
        out_shape=[
            jax.ShapeDtypeStruct((rows, pairs * 2 * HD), bf16),
            jax.ShapeDtypeStruct((pairs, 2, rows), f32),
        ],
        compiler_params=pltpu.CompilerParams(vmem_limit_bytes=48 << 20),
        cost_estimate=cost(pairs * rows * keys * 8 * HD * 8, pairs * (keys + rows) * 12 * HD),
        name="attend",
    )(row_at.reshape(1, -1), key_mark, near, far)


def attend_back_kernel(row_ref, key_ref, near_ref, far_ref, grad_ref, log_ref, *rest):
    out_ref = rest[-1]
    rows = grad_ref.shape[0]
    allowed = key_ref[...] <= row_ref[...]
    grad_query, grad_key, grad_value = [], [], []
    for h in range(2):
        query, key, value = head_parts(near_ref, far_ref, h)
        grad = grad_ref[:, h * HD : (h + 1) * HD]
        scores = contract(key, query, ((1,), (1,)))
        probs = jnp.where(allowed, jnp.exp(scores - log_ref[0, h : h + 1, :]), 0.0)
        grad_probs = contract(value, grad, ((1,), (1,)))
        centre = jnp.sum(probs * grad_probs, axis=0, keepdims=True)
        grad_scores = (probs * (grad_probs - centre)).astype(bf16)
        grad_query.append(contract(key, grad_scores, ((0,), (0,))))
        grad_key.append(contract(grad_scores, query, ((1,), (0,))).astype(bf16))
        grad_value.append(contract(probs.astype(bf16), grad, ((1,), (0,))).astype(bf16))
    turned = jnp.concatenate(grad_query, axis=0).T.astype(bf16)
    out_ref[:rows, : 2 * HD] = (turned.astype(f32) * HD ** (-0.5)).astype(bf16)
    out_ref[rows:, : 2 * HD] = jnp.zeros((out_ref.shape[0] - rows, 2 * HD), bf16)
    out_ref[:, 2 * HD : 4 * HD] = jnp.concatenate(grad_key, axis=1)
    out_ref[:, 4 * HD :] = jnp.concatenate(grad_value, axis=1)


def attend_back(near, far, grad, logs, row_at, key_mark, held, part, step, steps, parts):
    rows = row_at.shape[0]
    keys = rows + far.shape[0]
    columns = near.shape[1]
    pairs = columns // (6 * HD)
    out_shape = jax.ShapeDtypeStruct((steps * keys, parts * columns), bf16)
    in_specs = [
        pl.BlockSpec((1, rows), lambda j: (0, 0)),
        pl.BlockSpec((keys, 1), lambda j: (0, 0)),
        pl.BlockSpec((rows, 6 * HD), lambda j: (0, j)),
        pl.BlockSpec((keys - rows, 6 * HD), lambda j: (0, j)),
        pl.BlockSpec((rows, 2 * HD), lambda j: (0, j)),
        pl.BlockSpec((1, 2, rows), lambda j: (j, 0, 0)),
    ]
    args = [row_at.reshape(1, -1), key_mark, near, far, grad, logs]
    if held is not None:
        in_specs.append(pl.BlockSpec(memory_space=pl.ANY))
        args.append(held)
    return pl.pallas_call(
        attend_back_kernel,
        grid=(pairs,),
        in_specs=in_specs,
        out_specs=pl.BlockSpec((keys, 6 * HD), lambda j: (step, j + part * pairs)),
        out_shape=out_shape,
        input_output_aliases={} if held is None else {6: 0},
        compiler_params=pltpu.CompilerParams(vmem_limit_bytes=48 << 20),
        cost_estimate=cost(pairs * rows * keys * 16 * HD * 8, pairs * (keys + rows) * 24 * HD),
        name="attend_back",
    )(*args)


def expand_kernel(two_ref, cot_ref, up_ref, down_ref, bias_ref, *rest):
    active_ref, grad_ref, sum_ref = rest[-3:]
    active, slope = gelu_pair(
        contract(two_ref[...], up_ref[...], ((1,), (0,))) + bias_ref[...]
    )
    active_ref[...] = active.astype(bf16)
    grad_up = (contract(cot_ref[...], down_ref[...], ((1,), (0,))) * slope).astype(bf16)
    grad_ref[...] = grad_up
    sum_ref[...] = jnp.sum(grad_up.astype(f32), axis=0, keepdims=True)


def expand(two, cot, up, down, bias, held, part, step, steps, parts):
    rows, width = two.shape
    columns = up.shape[1]
    block = min(512, columns)
    count = columns // block
    in_specs = [
        pl.BlockSpec((rows, width), lambda j: (0, 0)),
        pl.BlockSpec((rows, width), lambda j: (0, 0)),
        pl.BlockSpec((width, block), lambda j: (0, j)),
        pl.BlockSpec((width, block), lambda j: (0, j)),
        pl.BlockSpec((1, block), lambda j: (0, j)),
    ]
    args = [two, cot, up, down, bias.reshape(1, -1)]
    if held is not None:
        in_specs += [pl.BlockSpec(memory_space=pl.ANY)] * 2
        args += list(held)
    whole = jax.ShapeDtypeStruct((steps * rows, parts * columns), bf16)
    return pl.pallas_call(
        expand_kernel,
        grid=(count,),
        in_specs=in_specs,
        out_specs=[
            pl.BlockSpec((rows, block), lambda j: (step, j + part * count)),
            pl.BlockSpec((rows, block), lambda j: (step, j + part * count)),
            pl.BlockSpec((1, block), lambda j: (0, j)),
        ],
        out_shape=[whole, whole, jax.ShapeDtypeStruct((1, columns), f32)],
        input_output_aliases={} if held is None else {5: 0, 6: 1},
        compiler_params=pltpu.CompilerParams(vmem_limit_bytes=48 << 20),
        cost_estimate=cost(4 * rows * width * columns, 4 * width * columns),
        name="expand",
    )(*args)


def times_kernel(a_ref, w_ref, bias_ref, scale_ref, out_ref):
    total = contract(a_ref[...], w_ref[...], ((1,), (0,)))
    out_ref[...] = ((total + bias_ref[...]) * scale_ref[...]).astype(bf16)


def times(rows_in, weight, first, columns, bias, scale):
    rows, width = rows_in.shape
    block = math.gcd(512, columns)
    start = first // block
    return pl.pallas_call(
        times_kernel,
        grid=(columns // block,),
        in_specs=[
            pl.BlockSpec((rows, width), lambda j: (0, 0)),
            pl.BlockSpec((width, block), lambda j: (0, start + j)),
            pl.BlockSpec((1, block), lambda j: (0, j)),
            pl.BlockSpec((1, block), lambda j: (0, j)),
        ],
        out_specs=pl.BlockSpec((rows, block), lambda j: (0, j)),
        out_shape=jax.ShapeDtypeStruct((rows, columns), bf16),
        compiler_params=pltpu.CompilerParams(vmem_limit_bytes=48 << 20),
        cost_estimate=cost(2 * rows * width * columns, 2 * width * columns),
        name="times",
    )(rows_in, weight, bias.reshape(1, -1), scale.reshape(1, -1))


def back_kernel(count, rows, *refs):
    mine_ref, other_ref = refs[2 * count :]
    total = contract(refs[0][...], refs[1][...], ((1,), (1,)))
    for i in range(1, count):
        total = total + contract(refs[2 * i][...], refs[2 * i + 1][...], ((1,), (1,)))
    for i in range(mine_ref.shape[0] // rows):
        mine_ref[i * rows : (i + 1) * rows, :] = total[2 * i * rows : (2 * i + 1) * rows]
        other_ref[i * rows : (i + 1) * rows, :] = total[(2 * i + 1) * rows : (2 * i + 2) * rows].astype(bf16)


def times_back(parts, rows, sets, depth, step):
    width = parts[0][2].shape[0]
    block = min(512, width)
    in_specs, args = [], []
    for left, left_block, weight, weight_block in parts:
        in_specs.append(pl.BlockSpec((2 * sets * rows, depth), lambda j, b=left_block: (step, b)))
        in_specs.append(pl.BlockSpec((block, depth), lambda j, b=weight_block: (j, b)))
        args += [left, weight]
    out_spec = pl.BlockSpec((sets * rows, block), lambda j: (0, j))
    return pl.pallas_call(
        functools.partial(back_kernel, len(parts), rows),
        grid=(width // block,),
        in_specs=in_specs,
        out_specs=[out_spec, out_spec],
        out_shape=[
            jax.ShapeDtypeStruct((sets * rows, width), f32),
            jax.ShapeDtypeStruct((sets * rows, width), bf16),
        ],
        compiler_params=pltpu.CompilerParams(vmem_limit_bytes=56 << 20),
        cost_estimate=cost(
            4 * sets * rows * depth * width * len(parts), 2 * depth * width * len(parts)
        ),
        name="times_back",
    )(*args)


def shards(
    hidden_in,
    counts,
    summary,
    query_weight,
    query_bias,
    key_weight,
    value_weight,
    value_bias,
    out_weight,
    out_bias,
    up_weight,
    up_bias,
    down_weight,
    down_bias,
    attn_gain,
    attn_shift,
    mlp_gain,
    mlp_shift,
    cotangent,
):
    micro_total = hidden_in.shape[0]
    rows = hidden_in.shape[1]
    groups = lax.axis_size("g")
    seq_len = rows * groups * 2
    spot = lax.axis_index(MP)
    cols = query_weight.shape[1]
    ff = up_weight.shape[1]
    micros = range(micro_total)
    quarters = range(groups)
    qk_scale = HD ** (-0.5)
    order = ring_blocks()
    back_order = jnp.argsort(order).astype(jnp.int32)
    near = 2 * rows
    core_axis = D // 2

    last = ()

    def turn(work, *args):
        nonlocal last
        args, last = lax.optimization_barrier((args, last))
        last = work(*args)
        return last

    steps = jnp.arange(rows, dtype=jnp.int32)
    place = []
    for d in quarters:
        base = spot - 2 * d
        twin = base + 1 - 2 * lax.axis_index("r")
        place += [base * rows + steps, twin * rows + steps]
    key_at = jnp.concatenate(place)
    row_at = key_at[:near]
    picker = (
        (row_at[:rows] - (seq_len - SUMM))[:, None] == jnp.arange(SUMM, dtype=jnp.int32)[None, :]
    ).astype(f32)

    join = lambda *parts: jnp.concatenate(parts)

    def by_heads(query, key, value):
        parts = [part.reshape(part.shape[:-1] + (-1, 1, 2 * HD)) for part in (query, key, value)]
        return jnp.concatenate(parts, axis=-2).reshape(query.shape[:-1] + (-1,))

    def start_rows(hidden):
        joined = hidden.astype(f32) + jnp.dot(picker, summary, precision=precise)
        normed, unit, scale = layer_norm(joined, attn_gain, attn_shift)
        return normed.astype(bf16), joined, unit, scale

    depth = query_weight.shape[0]

    def start_weights(query, key, value, out, query_add, value_add, up_add):
        adds = jnp.concatenate((by_heads(query_add, jnp.zeros_like(query_add), value_add), up_add))
        adds = jnp.concatenate((adds, jnp.zeros((64 * cols - adds.shape[0],), bf16))).reshape(16, -1)
        weights = jnp.concatenate((by_heads(query, key, value), out.T), axis=1)
        return weights, jnp.concatenate((weights, adds)), adds

    def middle_rows(joined, mine, other):
        mixed = joined + (mine + other.astype(f32)) + bias_out
        normed, unit, scale = layer_norm(mixed, mlp_gain, mlp_shift)
        return normed.astype(bf16), mixed, unit, scale

    def low_rows(left, right):
        return inner_rows(left, right).astype(bf16)

    ones = jnp.ones((cols,), f32)
    scale_qkv = by_heads(ones * qk_scale, ones, ones)
    bias_out = out_bias.astype(f32)
    bias_down = down_bias.astype(f32)

    first = [turn(start_rows, hidden_in[0])]
    near_swaps = [swap_pair(first[0][0])]
    far_shifts = [[shift_up(first[0][0], d) for d in range(1, groups)]]

    attn_own, attn_more, adds = turn(
        start_weights, query_weight, key_weight, value_weight, out_weight, query_bias, value_bias, up_bias
    )
    attn_full = [lax.all_gather(attn_own, DP, axis=0, tiled=True)]
    down_own = turn(jnp.transpose, down_weight)
    gathers = [RingGather(down_own)]
    first += [turn(start_rows, hidden_in[m]) for m in micros[1:]]

    def mark_keys(positions, used):
        return [
            jnp.where(live_keys(positions, seq_len, used[m, 0]), positions, 1 << 30).reshape(-1, 1)
            for m in micros
        ]

    key_mark = turn(mark_keys, key_at, counts)
    lows = [first[m][0] for m in micros]

    def pick_rows(values):
        picked = pick_columns(values.reshape(-1, D), order)
        return [picked[m * rows : (m + 1) * rows] for m in micros]

    cots = turn(pick_rows, cotangent)

    def first_two(mine, other, *_):
        return jnp.concatenate((mine, other))

    def split_adds(*turned):
        parts = [adds.reshape(-1)] + [part[depth:].reshape(-1) for part in turned]
        weights = [part[:depth] for part in turned]
        return weights, [part[: 3 * cols].astype(f32) for part in parts], [
            part[3 * cols : 3 * cols + ff].astype(f32) for part in parts
        ]


    def project(rows_in, weight, bias):
        return times(rows_in, weight, 0, 3 * cols, bias, scale_qkv)

    near_parts = [[None] * groups for m in micros]
    far_rows = [None] * micro_total
    far_parts = [[None] * groups for m in micros]
    logs = [[None] * groups for m in micros]
    attended = [[None] * groups for m in micros]
    out_parts = [None] * micro_total
    second = [None] * micro_total
    two_swaps = [None] * micro_total

    def near_work(m, d):
        near_parts[m][d] = turn(project, near_rows[m], attn_full[d], bias_qkv[d])

    def far_work(m, d):
        far_parts[m][d] = turn(project, far_rows[m], attn_full[d], bias_qkv[d])

    def attend_work(m, d):
        attended[m][d], logs[m][d] = turn(
            lambda n, f: attend(n, f, row_at, key_mark[m]), near_parts[m][d], far_parts[m][d]
        )

    def out_work(m):
        mine, other = turn(
            lambda *args: times_back(
                [(args[d], 0, args[groups + d], 3) for d in quarters], rows, 1, cols, 0
            ),
            *attended[m],
            *attn_full,
        )
        out_parts[m] = (mine, swap_pair(other))

    def middle_work(m):
        second[m] = turn(middle_rows, first[m][1], *out_parts[m])
        two_swaps[m] = swap_pair(second[m][0])

    bias_qkv = [adds.reshape(-1)[: 3 * cols].astype(f32)]
    near_rows = [
        turn(first_two, lows[0], near_swaps[0], *far_shifts[0], gathers[0].right, gathers[0].left)
    ]
    far_swaps = [[swap_pair(after(block, near_rows[0])) for block in far_shifts[0]]]
    attn_turned = [turn_up(after(attn_more, near_rows[0]), d) for d in range(1, groups)]
    gathers[0].advance(turn)
    near_work(0, 0)

    def far_join(m, *gate):
        blocks = [block for d in range(groups - 1) for block in (far_shifts[m][d], far_swaps[m][d])]
        count = len(blocks)
        far_rows[m] = turn(lambda *parts: jnp.concatenate(parts[:count]), *blocks, *gate)

    far_join(0, *attn_turned, gathers[0].right, gathers[0].left)
    cot_swaps = [swap_pair(after(cots[0], far_swaps[0], attn_turned))]
    for m in micros[1:]:
        low = after(lows[m], far_swaps[0], attn_turned)
        near_swaps.append(swap_pair(low))
        far_shifts.append([shift_up(low, d) for d in range(1, groups)])
    attn_shards, bias_qkv, bias_up = turn(split_adds, *attn_turned)
    attn_shards = after(attn_shards, near_parts[0][0])
    attn_full += [lax.all_gather(shard, DP, axis=0, tiled=True) for shard in attn_shards]
    far_work(0, 0)
    attend_work(0, 0)
    gathers[0].across(turn)
    for m in micros[1:]:
        near_rows.append(turn(first_two, lows[m], near_swaps[m], *far_shifts[m], cot_swaps[0]))
        far_swaps.append([swap_pair(after(block, near_rows[m])) for block in far_shifts[m]])
    up_turned = [turn_up(after(up_weight, far_swaps[-1]), d) for d in range(1, groups)]
    for d in range(1, groups):
        near_work(0, d)
        far_work(0, d)
        attend_work(0, d)
    up_full = [lax.all_gather(after(up_weight, near_parts[0][-1]), DP, axis=0, tiled=True)]
    out_work(0)
    for m in micros[1:]:
        near_work(m, 0)
    far_join(1)
    far_work(1, 0)
    attend_work(1, 0)
    down_turned = [turn_up(after(down_own, up_turned, far_parts[1][0]), d) for d in range(1, groups)]
    middle_work(0)
    cot_swaps += [swap_pair(after(cots[m], up_turned, second[0])) for m in micros[1:]]
    up_full += [lax.all_gather(after(shard, attended[1][0]), DP, axis=0, tiled=True) for shard in up_turned]
    for d in range(1, groups):
        near_work(1, d)
        far_work(1, d)
    down_full = [gathers[0].finish(turn)]
    for d in range(1, groups):
        attend_work(1, d)
    gathers += [RingGather(after(shard, attended[1][-1])) for shard in down_turned]
    out_work(1)
    cot_pair = [turn(join, cots[0], cot_swaps[0])]

    two_pair = [None] * micro_total
    held = None
    up_sums = [[None] * groups for m in micros]

    def two_work(m):
        two_pair[m] = turn(join, second[m][0], two_swaps[m])

    def hidden_units(m, d):
        nonlocal held
        *held, up_sums[m][d] = turn(
            lambda *args: expand(*args[:5], args[5:] or None, d, m, micro_total, groups),
            two_pair[m],
            cot_pair[m],
            up_full[d],
            down_full[d],
            bias_up[d],
            *(held or ()),
        )

    def back_work(m, left, weights):
        mine, other = turn(
            lambda left, *weights: times_back(
                [(left, d, weights[d], 0) for d in quarters], rows, 1, ff, m
            ),
            left,
            *weights,
        )
        return mine, other

    def middle_back(cot, mine, other, unit, scale, *_):
        grad_two = mine + other.astype(f32)
        grad_layer = cot.astype(f32)
        grad_mixed = grad_layer + norm_back(grad_two, unit, scale, mlp_gain)
        sums = jnp.stack(
            (
                jnp.sum(grad_mixed, axis=0),
                jnp.sum(grad_layer, axis=0),
                jnp.sum(grad_two * unit, axis=0),
                jnp.sum(grad_two, axis=0),
            )
        )
        return grad_mixed.astype(bf16), grad_mixed, sums

    third = [None] * micro_total
    mixed_swaps = [None] * micro_total
    mixed_pair = [None] * micro_total
    outputs = [None] * micro_total

    def third_work(m, parts, *gate):
        third[m] = turn(middle_back, cotangent[m], *parts, second[m][2], second[m][3], *gate)
        mixed_swaps[m] = swap_pair(third[m][0])

    def layer_work(m, parts):
        outputs[m] = turn(
            lambda mixed, mine, other: (
                mixed + pick_columns(mine + other.astype(f32), back_order) + bias_down
            ).astype(bf16),
            second[m][1],
            *parts,
        )

    def mixed_work(m):
        mixed_pair[m] = turn(join, third[m][0], mixed_swaps[m])

    two_work(0)
    hidden_units(0, 0)
    for gather in gathers[1:]:
        gather.advance(turn)
    middle_work(1)
    for gather in gathers[1:]:
        gather.across(turn)
    down_full += [gather.finish(turn) for gather in gathers[1:]]
    for d in range(1, groups):
        hidden_units(0, d)
    grad_first = back_work(0, held[1], up_full)
    grad_first = (grad_first[0], swap_pair(grad_first[1]))
    two_work(1)
    cot_pair += [turn(join, cots[m], cot_swaps[m]) for m in micros[1:]]
    hidden_units(1, 0)
    down_first = back_work(0, held[0], down_full)
    third_work(0, grad_first)
    for d in range(1, groups):
        hidden_units(1, d)
    grad_second = back_work(1, held[1], up_full)
    grad_second = (grad_second[0], swap_pair(grad_second[1]))
    active_all, grad_up_all = held
    down_second = back_work(1, active_all, down_full)
    mixed_work(0)
    third_work(1, grad_second)

    cot_all = turn(join, *cot_pair)
    down_other = turn(lambda left, right: low_rows(left[:, core_axis:], right), cot_all, active_all)
    down_other = swap_core(down_other)
    two_all = turn(join, *two_pair)
    up_sum = turn(low_rows, two_all, grad_up_all)
    down_first = (down_first[0], swap_pair(after(down_first[1], up_sum)))
    down_second = (down_second[0], swap_pair(after(down_second[1], up_sum)))
    up_part = lax.psum_scatter(up_sum, DP, scatter_dimension=0, tiled=True)
    down_sum = turn(
        lambda left, right, other: (
            inner_rows(left[:, :core_axis], right) + other.astype(f32)
        ).astype(bf16),
        cot_all,
        active_all,
        down_other,
    )
    down_ring = RingScatter(down_sum, down_own.shape[0])
    mixed_work(1)

    grads = None
    back_parts = [[None] * groups for m in micros]

    def grad_work(m):
        return [
            turn(lambda g, w: times(g, w, 3 * cols, cols, jnp.zeros((cols,), f32), ones), mixed_pair[m], weight)
            for weight in attn_full
        ]

    def attend_back_work(m, d, grad):
        nonlocal grads
        grads = turn(
            lambda n, f, g, l, h: attend_back(
                n, f, g, l, row_at, key_mark[m], h, d, m, micro_total, groups
            ),
            near_parts[m][d],
            far_parts[m][d],
            grad,
            logs[m][d],
            grads,
        )

    def normed_work(m, set_at):
        mine, other = turn(
            lambda left, *weights: times_back(
                [(left, d, weights[d], 0) for d in quarters], rows, 1, 3 * cols, m * groups + set_at
            ),
            grads,
            *attn_full,
        )
        back_parts[m][set_at] = (mine, swap_pair(other))

    grad = grad_work(0)
    for d in quarters:
        attend_back_work(0, d, grad[d])
    attended_all = turn(
        lambda _, __, *parts: jnp.concatenate(
            [jnp.concatenate(parts[m * groups : (m + 1) * groups], axis=1) for m in micros]
        ),
        down_first[1],
        down_second[1],
        *[part for m in micros for part in attended[m]],
    )
    mixed_all = turn(join, *mixed_pair)
    out_sum = turn(low_rows, mixed_all, attended_all)
    out_part = lax.psum_scatter(after(out_sum, up_part), DP, scatter_dimension=0, tiled=True)

    def send_parts(part, size):
        parts = turn(lambda part: [part[:, d * size : (d + 1) * size] for d in quarters], part)
        return [parts[0]] + [turn_down(parts[d], d) for d in range(1, groups)]

    def collect(parts):
        return turn(lambda *parts: sum(part.astype(f32) for part in parts), *parts)

    def far_sum(mine, other):
        return (mine + other.astype(f32)).astype(bf16)

    def last_back(grad_mixed, mine, other, unit, scale, *far):
        grad_normed = mine + other.astype(f32)
        for block in far:
            grad_normed = grad_normed + block.astype(f32)
        grad_joined = grad_mixed + norm_back(grad_normed, unit, scale, attn_gain)
        sums = jnp.stack((jnp.sum(grad_normed * unit, axis=0), jnp.sum(grad_normed, axis=0)))
        return grad_joined, sums, jnp.dot(picker.T, grad_joined, precision=precise)

    shifts = [None] * micro_total
    fourth = [None] * micro_total

    def far_back(m):
        blocks = [turn(far_sum, *back_parts[m][d]) for d in range(1, groups)]
        shifts[m] = [shift_down(blocks[d - 1], d) for d in range(1, groups)]

    def last_work(m):
        fourth[m] = turn(
            last_back, third[m][1], *back_parts[m][0], first[m][2], first[m][3], *shifts[m]
        )

    for d in range(1, groups):
        normed_work(0, d)
    normed_work(0, 0)
    far_back(0)
    grad = grad_work(1)
    attend_back_work(1, 0, grad[0])
    down_ring.advance(turn)
    up_sent = send_parts(up_part, ff)
    for d in range(1, groups):
        attend_back_work(1, d, grad[d])
    for d in range(1, groups):
        normed_work(1, d)
    normed_all = turn(
        lambda *parts: jnp.concatenate(parts),
        *[part for m in micros for part in (near_rows[m], far_rows[m])],
    )
    normed_work(1, 0)
    grad_upw = collect(up_sent)
    down_part = down_ring.finish(turn)
    qkv_sum = turn(
        low_rows, *after((normed_all, grads), out_part, shifts[0], [part[1] for part in back_parts[1][1:]])
    )

    def own_blocks(total, first_block):
        count = order.shape[0] // 2
        return jnp.concatenate(
            [
                lax.dynamic_slice_in_dim(total, order[first_block + i] * depth, depth, 0)
                for i in range(count)
            ]
        )

    qkv_other = swap_core(turn(lambda total: own_blocks(total, order.shape[0] // 2), qkv_sum))
    far_back(1)
    qkv_mine = turn(
        lambda total, other: (own_blocks(total, 0).astype(f32) + other.astype(f32)).astype(bf16),
        qkv_sum,
        qkv_other,
    )
    qkv_ring = RingScatter(qkv_mine, depth)
    held_sum = turn(lambda grads: jnp.sum(grads.astype(f32), axis=0), grads)
    layer_work(0, down_first)
    qkv_ring.advance(turn)
    down_sent = send_parts(down_part, ff)
    last_work(0)
    layer_work(1, down_second)
    last_work(1)
    input_grads = [fourth[m][0] for m in micros]

    held_sum = held_sum.reshape(groups, -1, 3, 2 * HD)
    parts = jnp.concatenate(
        (
            held_sum[:, :, 0].reshape(groups, cols),
            held_sum[:, :, 2].reshape(groups, cols),
            jnp.concatenate([sum(up_sums[m][d] for m in micros) for d in quarters]),
        ),
        axis=1,
    )
    places = jnp.arange(2 * groups, dtype=jnp.int32)
    slots = jnp.zeros((2 * groups, parts.shape[1]), f32)
    for d in quarters:
        slots = slots + jnp.where(
            places[:, None] == (spot - 2 * d) % (2 * groups), parts[d][None], 0.0
        )
    small = jnp.concatenate(
        (
            sum(third[m][2] for m in micros),
            sum(fourth[m][1] for m in micros),
            sum(fourth[m][2] for m in micros),
            slots.reshape(-1, D),
        )
    )
    small = turn(
        lambda small: jnp.concatenate((small, jnp.zeros((-small.shape[0] % 16, D), f32))), small
    )
    summing = SumAll(small, turn)
    qkv_part = qkv_ring.finish(turn)
    qkv_sent = send_parts(qkv_part, 3 * cols)
    out_sent = send_parts(out_part, cols)
    while summing.left > 1:
        summing.advance(turn)
    grad_down = collect(down_sent).T
    small = summing.finish(turn)
    row_total = [small[i] for i in (0, 1, 4, 5, 2, 3)] + [small[6 : 6 + SUMM]]
    slots = small[6 + SUMM : 6 + SUMM + slots.size // D].reshape(slots.shape)
    bias_grad = lax.dynamic_index_in_dim(slots, spot, 0, keepdims=False)
    grad_out = collect(out_sent).T
    grad_qkv = collect(qkv_sent)
    grad_qkv = grad_qkv.reshape(grad_qkv.shape[0], -1, 3, 2 * HD)
    grad_query, grad_key, grad_value = (grad_qkv[:, :, i].reshape(-1, cols) for i in range(3))
    return (
        jnp.stack(outputs),
        jnp.stack(input_grads),
        row_total[6],
        grad_query,
        bias_grad[:cols],
        grad_key,
        grad_value,
        bias_grad[cols : 2 * cols],
        grad_out,
        row_total[0],
        grad_upw,
        bias_grad[2 * cols :],
        grad_down,
        row_total[1],
        row_total[2],
        row_total[3],
        row_total[4],
        row_total[5],
    )


def solution(mesh):
    data = mesh.shape["dp"]
    model = mesh.shape["mp"]
    fine = Mesh(mesh.devices.reshape(data // 2, 2, model // 2, 2), ALL)
    rows_spec = P(None, ALL, None)
    wide_spec = P(DP, MP)
    tall_spec = P(MP, DP)
    in_specs = (
        rows_spec,
        P(None, DP),
        P(),
        wide_spec,
        P(MP),
        wide_spec,
        wide_spec,
        P(MP),
        tall_spec,
        P(),
        wide_spec,
        P(MP),
        tall_spec,
        P(),
        P(),
        P(),
        P(),
        P(),
        rows_spec,
    )
    out_specs = (
        rows_spec,
        rows_spec,
        P(),
        wide_spec,
        P(MP),
        wide_spec,
        wide_spec,
        P(MP),
        tall_spec,
        P(),
        wide_spec,
        P(MP),
        tall_spec,
        P(),
        P(),
        P(),
        P(),
        P(),
    )
    return jax.shard_map(shards, mesh=fine, in_specs=in_specs, out_specs=out_specs, check_vma=False)
```

```python
import functools
import math

import jax
import jax.numpy as jnp
from jax import lax
from jax.experimental import pallas as pl
from jax.experimental.pallas import tpu as pltpu
from jax.sharding import Mesh
from jax.sharding import PartitionSpec as P

D = 2048
HD = 64
SUMM = 50

precise = lax.Precision.HIGHEST
gelu_coef = math.sqrt(2.0 / math.pi)
bf16 = jnp.bfloat16
f32 = jnp.float32
DP = ("xy", "c")
MP = ("g", "r")
ALL = ("xy", "c", "g", "r")


def gelu_pair(v):
    inner = gelu_coef * (v + 0.044715 * v * v * v)
    tangent = jnp.tanh(inner)
    half = 0.5 * (1.0 + tangent)
    slope = half + 0.5 * v * (1.0 - tangent * tangent) * gelu_coef * (1.0 + 3.0 * 0.044715 * v * v)
    return v * half, slope


def layer_norm(values_in, gain_vec, shift_vec):
    centred = values_in - jnp.mean(values_in, axis=-1, keepdims=True)
    spread = jnp.mean(centred * centred, axis=-1, keepdims=True)
    scaled = lax.rsqrt(spread + 1e-05)
    unit_rows = centred * scaled
    return (unit_rows * gain_vec + shift_vec, unit_rows, scaled)


def norm_back(grad_out, unit_rows, scaled, gain_vec):
    weighted = grad_out * gain_vec
    return scaled * (
        weighted
        - jnp.mean(weighted, axis=-1, keepdims=True)
        - unit_rows * jnp.mean(weighted * unit_rows, axis=-1, keepdims=True)
    )


def dense(left_side, right_side):
    return jnp.dot(left_side, right_side, preferred_element_type=f32)


def times_t(left_side, right_side):
    return lax.dot_general(left_side, right_side, (((1,), (1,)), ((), ())), preferred_element_type=f32)


def inner_rows(left_side, right_side):
    return lax.dot_general(left_side, right_side, (((0,), (0,)), ((), ())), preferred_element_type=f32)


def live_keys(positions, seq_len, item_count):
    slot_ids = positions - (seq_len - SUMM)
    return (
        (positions >= SUMM) & (slot_ids < 0)
        | (positions >= 0) & (positions < item_count)
        | (slot_ids >= 0) & (slot_ids < item_count)
    )


def swap_pair(values):
    return lax.ppermute(values, "r", [(0, 1), (1, 0)])


def swap_core(values):
    return lax.ppermute(values, "c", [(0, 1), (1, 0)])


def shift_up(values, step):
    size = lax.axis_size("g")
    return lax.ppermute(values, "g", [(i, i + step) for i in range(size - step)])


def shift_down(values, step):
    size = lax.axis_size("g")
    return lax.ppermute(values, "g", [(i + step, i) for i in range(size - step)])


def turn_up(values, step):
    size = lax.axis_size("g")
    return lax.ppermute(values, "g", [(i, (i + step) % size) for i in range(size)])


def turn_down(values, step):
    size = lax.axis_size("g")
    return lax.ppermute(values, "g", [((i + step) % size, i) for i in range(size)])


def cost(work, size):
    return pl.CostEstimate(flops=int(1 * work), bytes_accessed=int(1 * size), transcendentals=0)


def after(values, *earlier):
    return lax.optimization_barrier((values, earlier))[0]


def ring_order():
    size = lax.axis_size("xy")
    return list(range(size // 2)) + list(range(size - 1, size // 2 - 1, -1))


def ring_step(values, way):
    order = ring_order()
    size = len(order)
    return lax.ppermute(values, "xy", [(order[i], order[(i + way) % size]) for i in range(size)])


def ring_blocks():
    order = ring_order()
    size = len(order)
    here = jnp.asarray([order.index(i) for i in range(size)], jnp.int32)[lax.axis_index("xy")]
    offsets = [0] + [way * step for step in range(1, size // 2) for way in (-1, 1)] + [size // 2]
    chips = jnp.asarray(order, jnp.int32)[(here + jnp.asarray(offsets, jnp.int32)) % size]
    core = lax.axis_index("c")
    return jnp.concatenate((2 * chips + core, 2 * chips + 1 - core))


class RingGather:
    def __init__(self, shard):
        self.blocks = [shard]
        self.right, self.left = ring_step(shard, 1), ring_step(shard, -1)
        self.steps = lax.axis_size("xy") // 2 - 1

    def advance(self, turn):
        while self.steps > 1:
            self.blocks += [self.right, self.left]
            self.right, self.left = ring_step(self.right, 1), ring_step(self.left, -1)
            self.steps -= 1
        self.blocks += [self.right, self.left]
        half = self.right.shape[0] // 2
        right, left = turn(lambda right, left: (right[:half], left[half:]), self.right, self.left)
        self.right, self.left = ring_step(right, 1), ring_step(left, -1)

    def across(self, turn):
        self.mine = turn(lambda *parts: jnp.concatenate(parts), *self.blocks, self.right, self.left)
        self.other = swap_core(self.mine)

    def finish(self, turn):
        return turn(lambda mine, other: jnp.concatenate((mine, other)), self.mine, self.other)


class RingScatter:
    def __init__(self, total, depth):
        self.steps = lax.axis_size("xy") // 2
        self.half = depth // 2
        self.blocks = [total[i * depth : (i + 1) * depth] for i in range(2 * self.steps)]
        self.first = True
        self.send(self.blocks[-1][: self.half], self.blocks[-1][self.half :])

    def send(self, right, left):
        self.steps -= 1
        self.came = (ring_step(right, 1), ring_step(left, -1))

    def add(self, right_block, left_block, right, left):
        def total(block, part):
            return (block.astype(f32) + part.astype(f32)).astype(bf16)

        if not self.first:
            return total(right_block, right), total(left_block, left)
        half = self.half
        return (
            jnp.concatenate((total(right_block[:half], right), right_block[half:])),
            jnp.concatenate((left_block[:half], total(left_block[half:], left))),
        )

    def advance(self, turn):
        right, left = self.blocks[2 * self.steps], self.blocks[2 * self.steps - 1]
        right, left = turn(self.add, right, left, *self.came)
        self.first = False
        self.send(right, left)

    def finish(self, turn):
        while self.steps > 0:
            self.advance(turn)

        def total(block, right, left):
            return (block.astype(f32) + right.astype(f32) + left.astype(f32)).astype(bf16)

        return turn(total, self.blocks[0], *self.came)


def move_block(order_ref, in_ref, out_ref):
    out_ref[...] = in_ref[...]


def pick_columns(values, order):
    rows, columns = values.shape
    width = columns // order.shape[0]
    return pl.pallas_call(
        move_block,
        grid_spec=pltpu.PrefetchScalarGridSpec(
            num_scalar_prefetch=1,
            grid=(order.shape[0],),
            in_specs=[pl.BlockSpec((rows, width), lambda j, order_ref: (0, order_ref[j]))],
            out_specs=pl.BlockSpec((rows, width), lambda j, order_ref: (0, j)),
        ),
        out_shape=jax.ShapeDtypeStruct(values.shape, values.dtype),
        cost_estimate=cost(0, 4 * values.size * values.dtype.itemsize),
        name="pick_columns",
    )(order, values)


class SumAll:
    def __init__(self, values, turn):
        half = values.shape[0] // 2
        core = lax.axis_index("c")
        self.total, other = turn(
            lambda values: (
                lax.dynamic_slice_in_dim(values, core * half, half, 0),
                lax.dynamic_slice_in_dim(values, (1 - core) * half, half, 0),
            ),
            values,
        )
        self.came = swap_core(other)
        self.ways = []
        for axis in ("xy", "r", "g"):
            size = lax.axis_size(axis)
            bit = 1
            while bit < size:
                self.ways.append((axis, [(i, i ^ bit) for i in range(size)]))
                bit *= 2
        self.left = len(self.ways)

    def advance(self, turn):
        self.total = turn(jnp.add, self.total, self.came)
        axis, pairs = self.ways[len(self.ways) - self.left]
        self.came = lax.ppermute(self.total, axis, pairs)
        self.left -= 1

    def finish(self, turn):
        while self.left > 0:
            self.advance(turn)
        self.total = turn(jnp.add, self.total, self.came)
        other = swap_core(self.total)
        low = lax.axis_index("c") == 0
        return turn(
            lambda total, other: jnp.where(
                low, jnp.concatenate((total, other)), jnp.concatenate((other, total))
            ),
            self.total,
            other,
        )


def contract(left, right, dims):
    return lax.dot_general(left, right, (dims, ((), ())), preferred_element_type=f32)


def head_parts(near_ref, far_ref, h):
    query = near_ref[:, h * HD : (h + 1) * HD]
    key = jnp.concatenate((near_ref[:, (2 + h) * HD : (3 + h) * HD], far_ref[:, (2 + h) * HD : (3 + h) * HD]))
    value = jnp.concatenate((near_ref[:, (4 + h) * HD : (5 + h) * HD], far_ref[:, (4 + h) * HD : (5 + h) * HD]))
    return query, key, value


def attend_kernel(row_ref, key_ref, near_ref, far_ref, out_ref, log_ref):
    allowed = key_ref[...] <= row_ref[...]
    outs = []
    for h in range(2):
        query, key, value = head_parts(near_ref, far_ref, h)
        scores = jnp.where(allowed, contract(key, query, ((1,), (1,))), -1e30)
        top = jnp.max(scores, axis=0, keepdims=True)
        powers = jnp.exp(scores - top)
        whole = jnp.sum(powers, axis=0, keepdims=True)
        outs.append(contract(value, powers.astype(bf16), ((0,), (0,))) / whole)
        log_ref[0, h : h + 1, :] = top + jnp.log(whole)
    out_ref[...] = jnp.concatenate(outs, axis=0).T.astype(bf16)


def attend(near, far, row_at, key_mark):
    rows = row_at.shape[0]
    keys = rows + far.shape[0]
    pairs = near.shape[1] // (6 * HD)
    return pl.pallas_call(
        attend_kernel,
        grid=(pairs,),
        in_specs=[
            pl.BlockSpec((1, rows), lambda j: (0, 0)),
            pl.BlockSpec((keys, 1), lambda j: (0, 0)),
            pl.BlockSpec((rows, 6 * HD), lambda j: (0, j)),
            pl.BlockSpec((keys - rows, 6 * HD), lambda j: (0, j)),
        ],
        out_specs=[
            pl.BlockSpec((rows, 2 * HD), lambda j: (0, j)),
            pl.BlockSpec((1, 2, rows), lambda j: (j, 0, 0)),
        ],
        out_shape=[
            jax.ShapeDtypeStruct((rows, pairs * 2 * HD), bf16),
            jax.ShapeDtypeStruct((pairs, 2, rows), f32),
        ],
        compiler_params=pltpu.CompilerParams(vmem_limit_bytes=48 << 20),
        cost_estimate=cost(pairs * rows * keys * 8 * HD * 8, pairs * (keys + rows) * 12 * HD),
        name="attend",
    )(row_at.reshape(1, -1), key_mark, near, far)


def attend_back_kernel(row_ref, key_ref, near_ref, far_ref, grad_ref, log_ref, *rest):
    out_ref = rest[-1]
    rows = grad_ref.shape[0]
    allowed = key_ref[...] <= row_ref[...]
    grad_query, grad_key, grad_value = [], [], []
    for h in range(2):
        query, key, value = head_parts(near_ref, far_ref, h)
        grad = grad_ref[:, h * HD : (h + 1) * HD]
        scores = contract(key, query, ((1,), (1,)))
        probs = jnp.where(allowed, jnp.exp(scores - log_ref[0, h : h + 1, :]), 0.0)
        grad_probs = contract(value, grad, ((1,), (1,)))
        centre = jnp.sum(probs * grad_probs, axis=0, keepdims=True)
        grad_scores = (probs * (grad_probs - centre)).astype(bf16)
        grad_query.append(contract(key, grad_scores, ((0,), (0,))))
        grad_key.append(contract(grad_scores, query, ((1,), (0,))).astype(bf16))
        grad_value.append(contract(probs.astype(bf16), grad, ((1,), (0,))).astype(bf16))
    turned = jnp.concatenate(grad_query, axis=0).T.astype(bf16)
    out_ref[:rows, : 2 * HD] = (turned.astype(f32) * HD ** (-0.5)).astype(bf16)
    out_ref[rows:, : 2 * HD] = jnp.zeros((out_ref.shape[0] - rows, 2 * HD), bf16)
    out_ref[:, 2 * HD : 4 * HD] = jnp.concatenate(grad_key, axis=1)
    out_ref[:, 4 * HD :] = jnp.concatenate(grad_value, axis=1)


def attend_back(near, far, grad, logs, row_at, key_mark, held, part, step, steps, parts):
    rows = row_at.shape[0]
    keys = rows + far.shape[0]
    columns = near.shape[1]
    pairs = columns // (6 * HD)
    out_shape = jax.ShapeDtypeStruct((steps * keys, parts * columns), bf16)
    in_specs = [
        pl.BlockSpec((1, rows), lambda j: (0, 0)),
        pl.BlockSpec((keys, 1), lambda j: (0, 0)),
        pl.BlockSpec((rows, 6 * HD), lambda j: (0, j)),
        pl.BlockSpec((keys - rows, 6 * HD), lambda j: (0, j)),
        pl.BlockSpec((rows, 2 * HD), lambda j: (0, j)),
        pl.BlockSpec((1, 2, rows), lambda j: (j, 0, 0)),
    ]
    args = [row_at.reshape(1, -1), key_mark, near, far, grad, logs]
    if held is not None:
        in_specs.append(pl.BlockSpec(memory_space=pl.ANY))
        args.append(held)
    return pl.pallas_call(
        attend_back_kernel,
        grid=(pairs,),
        in_specs=in_specs,
        out_specs=pl.BlockSpec((keys, 6 * HD), lambda j: (step, j + part * pairs)),
        out_shape=out_shape,
        input_output_aliases={} if held is None else {6: 0},
        compiler_params=pltpu.CompilerParams(vmem_limit_bytes=48 << 20),
        cost_estimate=cost(pairs * rows * keys * 16 * HD * 8, pairs * (keys + rows) * 24 * HD),
        name="attend_back",
    )(*args)


def expand_kernel(two_ref, cot_ref, up_ref, down_ref, bias_ref, *rest):
    active_ref, grad_ref, sum_ref = rest[-3:]
    active, slope = gelu_pair(
        contract(two_ref[...], up_ref[...], ((1,), (0,))) + bias_ref[...]
    )
    active_ref[...] = active.astype(bf16)
    grad_up = (contract(cot_ref[...], down_ref[...], ((1,), (0,))) * slope).astype(bf16)
    grad_ref[...] = grad_up
    sum_ref[...] = jnp.sum(grad_up.astype(f32), axis=0, keepdims=True)


def expand(two, cot, up, down, bias, held, part, step, steps, parts):
    rows, width = two.shape
    columns = up.shape[1]
    block = min(512, columns)
    count = columns // block
    in_specs = [
        pl.BlockSpec((rows, width), lambda j: (0, 0)),
        pl.BlockSpec((rows, width), lambda j: (0, 0)),
        pl.BlockSpec((width, block), lambda j: (0, j)),
        pl.BlockSpec((width, block), lambda j: (0, j)),
        pl.BlockSpec((1, block), lambda j: (0, j)),
    ]
    args = [two, cot, up, down, bias.reshape(1, -1)]
    if held is not None:
        in_specs += [pl.BlockSpec(memory_space=pl.ANY)] * 2
        args += list(held)
    whole = jax.ShapeDtypeStruct((steps * rows, parts * columns), bf16)
    return pl.pallas_call(
        expand_kernel,
        grid=(count,),
        in_specs=in_specs,
        out_specs=[
            pl.BlockSpec((rows, block), lambda j: (step, j + part * count)),
            pl.BlockSpec((rows, block), lambda j: (step, j + part * count)),
            pl.BlockSpec((1, block), lambda j: (0, j)),
        ],
        out_shape=[whole, whole, jax.ShapeDtypeStruct((1, columns), f32)],
        input_output_aliases={} if held is None else {5: 0, 6: 1},
        compiler_params=pltpu.CompilerParams(vmem_limit_bytes=48 << 20),
        cost_estimate=cost(4 * rows * width * columns, 4 * width * columns),
        name="expand",
    )(*args)


def times_kernel(a_ref, w_ref, bias_ref, scale_ref, out_ref):
    total = contract(a_ref[...], w_ref[...], ((1,), (0,)))
    out_ref[...] = ((total + bias_ref[...]) * scale_ref[...]).astype(bf16)


def times(rows_in, weight, first, columns, bias, scale):
    rows, width = rows_in.shape
    block = math.gcd(512, columns)
    start = first // block
    return pl.pallas_call(
        times_kernel,
        grid=(columns // block,),
        in_specs=[
            pl.BlockSpec((rows, width), lambda j: (0, 0)),
            pl.BlockSpec((width, block), lambda j: (0, start + j)),
            pl.BlockSpec((1, block), lambda j: (0, j)),
            pl.BlockSpec((1, block), lambda j: (0, j)),
        ],
        out_specs=pl.BlockSpec((rows, block), lambda j: (0, j)),
        out_shape=jax.ShapeDtypeStruct((rows, columns), bf16),
        compiler_params=pltpu.CompilerParams(vmem_limit_bytes=48 << 20),
        cost_estimate=cost(2 * rows * width * columns, 2 * width * columns),
        name="times",
    )(rows_in, weight, bias.reshape(1, -1), scale.reshape(1, -1))


def back_kernel(count, rows, *refs):
    mine_ref, other_ref = refs[2 * count :]
    total = contract(refs[0][...], refs[1][...], ((1,), (1,)))
    for i in range(1, count):
        total = total + contract(refs[2 * i][...], refs[2 * i + 1][...], ((1,), (1,)))
    for i in range(mine_ref.shape[0] // rows):
        mine_ref[i * rows : (i + 1) * rows, :] = total[2 * i * rows : (2 * i + 1) * rows]
        other_ref[i * rows : (i + 1) * rows, :] = total[(2 * i + 1) * rows : (2 * i + 2) * rows].astype(bf16)


def times_back(parts, rows, sets, depth, step):
    width = parts[0][2].shape[0]
    block = min(512, width)
    in_specs, args = [], []
    for left, left_block, weight, weight_block in parts:
        in_specs.append(pl.BlockSpec((2 * sets * rows, depth), lambda j, b=left_block: (step, b)))
        in_specs.append(pl.BlockSpec((block, depth), lambda j, b=weight_block: (j, b)))
        args += [left, weight]
    out_spec = pl.BlockSpec((sets * rows, block), lambda j: (0, j))
    return pl.pallas_call(
        functools.partial(back_kernel, len(parts), rows),
        grid=(width // block,),
        in_specs=in_specs,
        out_specs=[out_spec, out_spec],
        out_shape=[
            jax.ShapeDtypeStruct((sets * rows, width), f32),
            jax.ShapeDtypeStruct((sets * rows, width), bf16),
        ],
        compiler_params=pltpu.CompilerParams(vmem_limit_bytes=56 << 20),
        cost_estimate=cost(
            4 * sets * rows * depth * width * len(parts), 2 * depth * width * len(parts)
        ),
        name="times_back",
    )(*args)


def shards(
    hidden_in,
    counts,
    summary,
    query_weight,
    query_bias,
    key_weight,
    value_weight,
    value_bias,
    out_weight,
    out_bias,
    up_weight,
    up_bias,
    down_weight,
    down_bias,
    attn_gain,
    attn_shift,
    mlp_gain,
    mlp_shift,
    cotangent,
):
    micro_total = hidden_in.shape[0]
    rows = hidden_in.shape[1]
    groups = lax.axis_size("g")
    seq_len = rows * groups * 2
    spot = lax.axis_index(MP)
    cols = query_weight.shape[1]
    ff = up_weight.shape[1]
    micros = range(micro_total)
    quarters = range(groups)
    qk_scale = HD ** (-0.5)
    order = ring_blocks()
    back_order = jnp.argsort(order).astype(jnp.int32)
    near = 2 * rows
    core_axis = D // 2

    last = ()

    def turn(work, *args):
        nonlocal last
        args, last = lax.optimization_barrier((args, last))
        last = work(*args)
        return last

    steps = jnp.arange(rows, dtype=jnp.int32)
    place = []
    for d in quarters:
        base = spot - 2 * d
        twin = base + 1 - 2 * lax.axis_index("r")
        place += [base * rows + steps, twin * rows + steps]
    key_at = jnp.concatenate(place)
    row_at = key_at[:near]
    picker = (
        (row_at[:rows] - (seq_len - SUMM))[:, None] == jnp.arange(SUMM, dtype=jnp.int32)[None, :]
    ).astype(f32)

    join = lambda *parts: jnp.concatenate(parts)

    def by_heads(query, key, value):
        parts = [part.reshape(part.shape[:-1] + (-1, 1, 2 * HD)) for part in (query, key, value)]
        return jnp.concatenate(parts, axis=-2).reshape(query.shape[:-1] + (-1,))

    def start_rows(hidden):
        joined = hidden.astype(f32) + jnp.dot(picker, summary, precision=precise)
        normed, unit, scale = layer_norm(joined, attn_gain, attn_shift)
        return normed.astype(bf16), joined, unit, scale

    depth = query_weight.shape[0]

    def start_weights(query, key, value, out, query_add, value_add, up_add):
        adds = jnp.concatenate((by_heads(query_add, jnp.zeros_like(query_add), value_add), up_add))
        adds = jnp.concatenate((adds, jnp.zeros((64 * cols - adds.shape[0],), bf16))).reshape(16, -1)
        weights = jnp.concatenate((by_heads(query, key, value), out.T), axis=1)
        return weights, jnp.concatenate((weights, adds)), adds

    def middle_rows(joined, mine, other):
        mixed = joined + (mine + other.astype(f32)) + bias_out
        normed, unit, scale = layer_norm(mixed, mlp_gain, mlp_shift)
        return normed.astype(bf16), mixed, unit, scale

    def low_rows(left, right):
        return inner_rows(left, right).astype(bf16)

    ones = jnp.ones((cols,), f32)
    scale_qkv = by_heads(ones * qk_scale, ones, ones)
    bias_out = out_bias.astype(f32)
    bias_down = down_bias.astype(f32)

    first = [turn(start_rows, hidden_in[0])]
    near_swaps = [swap_pair(first[0][0])]
    far_shifts = [[shift_up(first[0][0], d) for d in range(1, groups)]]

    attn_own, attn_more, adds = turn(
        start_weights, query_weight, key_weight, value_weight, out_weight, query_bias, value_bias, up_bias
    )
    attn_full = [lax.all_gather(attn_own, DP, axis=0, tiled=True)]
    down_own = turn(jnp.transpose, down_weight)
    gathers = [RingGather(down_own)]
    first += [turn(start_rows, hidden_in[m]) for m in micros[1:]]

    def mark_keys(positions, used):
        return [
            jnp.where(live_keys(positions, seq_len, used[m, 0]), positions, 1 << 30).reshape(-1, 1)
            for m in micros
        ]

    key_mark = turn(mark_keys, key_at, counts)
    lows = [first[m][0] for m in micros]

    def pick_rows(values):
        picked = pick_columns(values.reshape(-1, D), order)
        return [picked[m * rows : (m + 1) * rows] for m in micros]

    cots = turn(pick_rows, cotangent)

    def first_two(mine, other, *_):
        return jnp.concatenate((mine, other))

    def split_adds(*turned):
        parts = [adds.reshape(-1)] + [part[depth:].reshape(-1) for part in turned]
        weights = [part[:depth] for part in turned]
        return weights, [part[: 3 * cols].astype(f32) for part in parts], [
            part[3 * cols : 3 * cols + ff].astype(f32) for part in parts
        ]


    def project(rows_in, weight, bias):
        return times(rows_in, weight, 0, 3 * cols, bias, scale_qkv)

    near_parts = [[None] * groups for m in micros]
    far_rows = [None] * micro_total
    far_parts = [[None] * groups for m in micros]
    logs = [[None] * groups for m in micros]
    attended = [[None] * groups for m in micros]
    out_parts = [None] * micro_total
    second = [None] * micro_total
    two_swaps = [None] * micro_total

    def near_work(m, d):
        near_parts[m][d] = turn(project, near_rows[m], attn_full[d], bias_qkv[d])

    def far_work(m, d):
        far_parts[m][d] = turn(project, far_rows[m], attn_full[d], bias_qkv[d])

    def attend_work(m, d):
        attended[m][d], logs[m][d] = turn(
            lambda n, f: attend(n, f, row_at, key_mark[m]), near_parts[m][d], far_parts[m][d]
        )

    def out_work(m):
        mine, other = turn(
            lambda *args: times_back(
                [(args[d], 0, args[groups + d], 3) for d in quarters], rows, 1, cols, 0
            ),
            *attended[m],
            *attn_full,
        )
        out_parts[m] = (mine, swap_pair(other))

    def middle_work(m):
        second[m] = turn(middle_rows, first[m][1], *out_parts[m])
        two_swaps[m] = swap_pair(second[m][0])

    bias_qkv = [adds.reshape(-1)[: 3 * cols].astype(f32)]
    near_rows = [
        turn(first_two, lows[0], near_swaps[0], *far_shifts[0], gathers[0].right, gathers[0].left)
    ]
    far_swaps = [[swap_pair(after(block, near_rows[0])) for block in far_shifts[0]]]
    attn_turned = [turn_up(after(attn_more, near_rows[0]), d) for d in range(1, groups)]
    gathers[0].advance(turn)
    near_work(0, 0)

    def far_join(m, *gate):
        blocks = [block for d in range(groups - 1) for block in (far_shifts[m][d], far_swaps[m][d])]
        count = len(blocks)
        far_rows[m] = turn(lambda *parts: jnp.concatenate(parts[:count]), *blocks, *gate)

    far_join(0, *attn_turned, gathers[0].right, gathers[0].left)
    for m in micros[1:]:
        low = after(lows[m], far_swaps[0], attn_turned)
        near_swaps.append(swap_pair(low))
        far_shifts.append([shift_up(low, d) for d in range(1, groups)])
    attn_shards, bias_qkv, bias_up = turn(split_adds, *attn_turned)
    attn_shards = after(attn_shards, near_parts[0][0])
    attn_full += [lax.all_gather(shard, DP, axis=0, tiled=True) for shard in attn_shards]
    far_work(0, 0)
    attend_work(0, 0)
    gathers[0].across(turn)
    for m in micros[1:]:
        near_rows.append(turn(first_two, lows[m], near_swaps[m], *far_shifts[m]))
        far_swaps.append([swap_pair(after(block, near_rows[m])) for block in far_shifts[m]])
    up_turned = [turn_up(after(up_weight, far_swaps[-1]), d) for d in range(1, groups)]
    cot_swaps = [swap_pair(after(cots[0], far_swaps[-1]))]
    for d in range(1, groups):
        near_work(0, d)
        far_work(0, d)
        attend_work(0, d)
    up_full = [lax.all_gather(after(up_weight, near_parts[0][-1]), DP, axis=0, tiled=True)]
    out_work(0)
    for m in micros[1:]:
        near_work(m, 0)
    far_join(1)
    far_work(1, 0)
    attend_work(1, 0)
    down_turned = [turn_up(after(down_own, up_turned, far_parts[1][0]), d) for d in range(1, groups)]
    middle_work(0)
    cot_swaps += [swap_pair(after(cots[m], up_turned, second[0])) for m in micros[1:]]
    for d in range(1, groups):
        near_work(1, d)
        far_work(1, d)
    up_full += [
        lax.all_gather(after(shard, near_parts[1][-1]), DP, axis=0, tiled=True) for shard in up_turned
    ]
    gathers += [RingGather(shard) for shard in down_turned]
    down_full = [gathers[0].finish(turn)]
    for d in range(1, groups):
        attend_work(1, d)
    out_work(1)
    cot_pair = [turn(join, cots[0], cot_swaps[0])]

    two_pair = [None] * micro_total
    held = None
    up_sums = [[None] * groups for m in micros]

    def two_work(m):
        two_pair[m] = turn(join, second[m][0], two_swaps[m])

    def hidden_units(m, d):
        nonlocal held
        *held, up_sums[m][d] = turn(
            lambda *args: expand(*args[:5], args[5:] or None, d, m, micro_total, groups),
            two_pair[m],
            cot_pair[m],
            up_full[d],
            down_full[d],
            bias_up[d],
            *(held or ()),
        )

    def back_work(m, left, weights):
        mine, other = turn(
            lambda left, *weights: times_back(
                [(left, d, weights[d], 0) for d in quarters], rows, 1, ff, m
            ),
            left,
            *weights,
        )
        return mine, other

    def middle_back(cot, mine, other, unit, scale, *_):
        grad_two = mine + other.astype(f32)
        grad_layer = cot.astype(f32)
        grad_mixed = grad_layer + norm_back(grad_two, unit, scale, mlp_gain)
        sums = jnp.stack(
            (
                jnp.sum(grad_mixed, axis=0),
                jnp.sum(grad_layer, axis=0),
                jnp.sum(grad_two * unit, axis=0),
                jnp.sum(grad_two, axis=0),
            )
        )
        return grad_mixed.astype(bf16), grad_mixed, sums

    third = [None] * micro_total
    mixed_swaps = [None] * micro_total
    mixed_pair = [None] * micro_total
    outputs = [None] * micro_total

    def third_work(m, parts, *gate):
        third[m] = turn(middle_back, cotangent[m], *parts, second[m][2], second[m][3], *gate)
        mixed_swaps[m] = swap_pair(third[m][0])

    def layer_work(m, parts):
        outputs[m] = turn(
            lambda mixed, mine, other: (
                mixed + pick_columns(mine + other.astype(f32), back_order) + bias_down
            ).astype(bf16),
            second[m][1],
            *parts,
        )

    def mixed_work(m):
        mixed_pair[m] = turn(join, third[m][0], mixed_swaps[m])

    two_work(0)
    hidden_units(0, 0)
    for gather in gathers[1:]:
        gather.advance(turn)
    middle_work(1)
    for gather in gathers[1:]:
        gather.across(turn)
    down_full += [gather.finish(turn) for gather in gathers[1:]]
    for d in range(1, groups):
        hidden_units(0, d)
    grad_first = back_work(0, held[1], up_full)
    grad_first = (grad_first[0], swap_pair(grad_first[1]))
    two_work(1)
    cot_pair += [turn(join, cots[m], cot_swaps[m]) for m in micros[1:]]
    hidden_units(1, 0)
    down_first = back_work(0, held[0], down_full)
    third_work(0, grad_first)
    for d in range(1, groups):
        hidden_units(1, d)
    grad_second = back_work(1, held[1], up_full)
    grad_second = (grad_second[0], swap_pair(grad_second[1]))
    active_all, grad_up_all = held
    down_second = back_work(1, active_all, down_full)
    mixed_work(0)
    third_work(1, grad_second)

    cot_all = turn(join, *cot_pair)
    down_other = turn(lambda left, right: low_rows(left[:, core_axis:], right), cot_all, active_all)
    down_other = swap_core(down_other)
    two_all = turn(join, *two_pair)
    up_sum = turn(low_rows, two_all, grad_up_all)
    down_first = (down_first[0], swap_pair(after(down_first[1], up_sum)))
    down_second = (down_second[0], swap_pair(after(down_second[1], up_sum)))
    up_part = lax.psum_scatter(up_sum, DP, scatter_dimension=0, tiled=True)
    down_sum = turn(
        lambda left, right, other: (
            inner_rows(left[:, :core_axis], right) + other.astype(f32)
        ).astype(bf16),
        cot_all,
        active_all,
        down_other,
    )
    down_ring = RingScatter(down_sum, down_own.shape[0])
    mixed_work(1)

    grads = None
    back_parts = [[None] * groups for m in micros]

    def grad_work(m):
        return [
            turn(lambda g, w: times(g, w, 3 * cols, cols, jnp.zeros((cols,), f32), ones), mixed_pair[m], weight)
            for weight in attn_full
        ]

    def attend_back_work(m, d, grad):
        nonlocal grads
        grads = turn(
            lambda n, f, g, l, h: attend_back(
                n, f, g, l, row_at, key_mark[m], h, d, m, micro_total, groups
            ),
            near_parts[m][d],
            far_parts[m][d],
            grad,
            logs[m][d],
            grads,
        )

    def normed_work(m, set_at):
        mine, other = turn(
            lambda left, *weights: times_back(
                [(left, d, weights[d], 0) for d in quarters], rows, 1, 3 * cols, m * groups + set_at
            ),
            grads,
            *attn_full,
        )
        back_parts[m][set_at] = (mine, swap_pair(other))

    grad = grad_work(0)
    for d in quarters:
        attend_back_work(0, d, grad[d])
    attended_all = turn(
        lambda _, __, *parts: jnp.concatenate(
            [jnp.concatenate(parts[m * groups : (m + 1) * groups], axis=1) for m in micros]
        ),
        down_first[1],
        down_second[1],
        *[part for m in micros for part in attended[m]],
    )
    mixed_all = turn(join, *mixed_pair)
    out_sum = turn(low_rows, mixed_all, attended_all)
    out_part = lax.psum_scatter(after(out_sum, up_part), DP, scatter_dimension=0, tiled=True)

    def send_parts(part, size):
        parts = turn(lambda part: [part[:, d * size : (d + 1) * size] for d in quarters], part)
        return [parts[0]] + [turn_down(parts[d], d) for d in range(1, groups)]

    def collect(parts):
        return turn(lambda *parts: sum(part.astype(f32) for part in parts), *parts)

    def far_sum(mine, other):
        return (mine + other.astype(f32)).astype(bf16)

    def last_back(grad_mixed, mine, other, unit, scale, *far):
        grad_normed = mine + other.astype(f32)
        for block in far:
            grad_normed = grad_normed + block.astype(f32)
        grad_joined = grad_mixed + norm_back(grad_normed, unit, scale, attn_gain)
        sums = jnp.stack((jnp.sum(grad_normed * unit, axis=0), jnp.sum(grad_normed, axis=0)))
        return grad_joined, sums, jnp.dot(picker.T, grad_joined, precision=precise)

    shifts = [None] * micro_total
    fourth = [None] * micro_total

    def far_back(m):
        blocks = [turn(far_sum, *back_parts[m][d]) for d in range(1, groups)]
        shifts[m] = [shift_down(blocks[d - 1], d) for d in range(1, groups)]

    def last_work(m):
        fourth[m] = turn(
            last_back, third[m][1], *back_parts[m][0], first[m][2], first[m][3], *shifts[m]
        )

    for d in range(1, groups):
        normed_work(0, d)
    normed_work(0, 0)
    far_back(0)
    grad = grad_work(1)
    attend_back_work(1, 0, grad[0])
    down_ring.advance(turn)
    up_sent = send_parts(up_part, ff)
    for d in range(1, groups):
        attend_back_work(1, d, grad[d])
    for d in range(1, groups):
        normed_work(1, d)
    normed_all = turn(
        lambda *parts: jnp.concatenate(parts),
        *[part for m in micros for part in (near_rows[m], far_rows[m])],
    )
    normed_work(1, 0)
    grad_upw = collect(up_sent)
    down_part = down_ring.finish(turn)
    qkv_sum = turn(
        low_rows, *after((normed_all, grads), out_part, shifts[0], [part[1] for part in back_parts[1][1:]])
    )

    def own_blocks(total, first_block):
        count = order.shape[0] // 2
        return jnp.concatenate(
            [
                lax.dynamic_slice_in_dim(total, order[first_block + i] * depth, depth, 0)
                for i in range(count)
            ]
        )

    qkv_other = swap_core(turn(lambda total: own_blocks(total, order.shape[0] // 2), qkv_sum))
    far_back(1)
    qkv_mine = turn(
        lambda total, other: (own_blocks(total, 0).astype(f32) + other.astype(f32)).astype(bf16),
        qkv_sum,
        qkv_other,
    )
    qkv_ring = RingScatter(qkv_mine, depth)
    held_sum = turn(lambda grads: jnp.sum(grads.astype(f32), axis=0), grads)
    layer_work(0, down_first)
    qkv_ring.advance(turn)
    down_sent = send_parts(down_part, ff)
    last_work(0)
    layer_work(1, down_second)
    last_work(1)
    input_grads = [fourth[m][0] for m in micros]

    held_sum = held_sum.reshape(groups, -1, 3, 2 * HD)
    parts = jnp.concatenate(
        (
            held_sum[:, :, 0].reshape(groups, cols),
            held_sum[:, :, 2].reshape(groups, cols),
            jnp.concatenate([sum(up_sums[m][d] for m in micros) for d in quarters]),
        ),
        axis=1,
    )
    places = jnp.arange(2 * groups, dtype=jnp.int32)
    slots = jnp.zeros((2 * groups, parts.shape[1]), f32)
    for d in quarters:
        slots = slots + jnp.where(
            places[:, None] == (spot - 2 * d) % (2 * groups), parts[d][None], 0.0
        )
    small = jnp.concatenate(
        (
            sum(third[m][2] for m in micros),
            sum(fourth[m][1] for m in micros),
            sum(fourth[m][2] for m in micros),
            slots.reshape(-1, D),
        )
    )
    small = turn(
        lambda small: jnp.concatenate((small, jnp.zeros((-small.shape[0] % 16, D), f32))), small
    )
    summing = SumAll(small, turn)
    qkv_part = qkv_ring.finish(turn)
    qkv_sent = send_parts(qkv_part, 3 * cols)
    out_sent = send_parts(out_part, cols)
    while summing.left > 1:
        summing.advance(turn)
    grad_down = collect(down_sent).T
    small = summing.finish(turn)
    row_total = [small[i] for i in (0, 1, 4, 5, 2, 3)] + [small[6 : 6 + SUMM]]
    slots = small[6 + SUMM : 6 + SUMM + slots.size // D].reshape(slots.shape)
    bias_grad = lax.dynamic_index_in_dim(slots, spot, 0, keepdims=False)
    grad_out = collect(out_sent).T
    grad_qkv = collect(qkv_sent)
    grad_qkv = grad_qkv.reshape(grad_qkv.shape[0], -1, 3, 2 * HD)
    grad_query, grad_key, grad_value = (grad_qkv[:, :, i].reshape(-1, cols) for i in range(3))
    return (
        jnp.stack(outputs),
        jnp.stack(input_grads),
        row_total[6],
        grad_query,
        bias_grad[:cols],
        grad_key,
        grad_value,
        bias_grad[cols : 2 * cols],
        grad_out,
        row_total[0],
        grad_upw,
        bias_grad[2 * cols :],
        grad_down,
        row_total[1],
        row_total[2],
        row_total[3],
        row_total[4],
        row_total[5],
    )


def solution(mesh):
    data = mesh.shape["dp"]
    model = mesh.shape["mp"]
    fine = Mesh(mesh.devices.reshape(data // 2, 2, model // 2, 2), ALL)
    rows_spec = P(None, ALL, None)
    wide_spec = P(DP, MP)
    tall_spec = P(MP, DP)
    in_specs = (
        rows_spec,
        P(None, DP),
        P(),
        wide_spec,
        P(MP),
        wide_spec,
        wide_spec,
        P(MP),
        tall_spec,
        P(),
        wide_spec,
        P(MP),
        tall_spec,
        P(),
        P(),
        P(),
        P(),
        P(),
        rows_spec,
    )
    out_specs = (
        rows_spec,
        rows_spec,
        P(),
        wide_spec,
        P(MP),
        wide_spec,
        wide_spec,
        P(MP),
        tall_spec,
        P(),
        wide_spec,
        P(MP),
        tall_spec,
        P(),
        P(),
        P(),
        P(),
        P(),
    )
    return jax.shard_map(shards, mesh=fine, in_specs=in_specs, out_specs=out_specs, check_vma=False)
```
